32 devices in a mesh: near: 2 (over x), row: 4 (over z), col: 4 (over y, core).
Axes of the slice: x: 2, y: 2, z: 4, core: 2. Of those that a mesh axis runs over, the one named last changes fastest.
Arguments:
- right_side: float32 [32, 512, 128], P(('near', 'row', 'col')), may hold values from -6 to 6
- start_guess: float32 [32, 512, 128], P(('near', 'row', 'col')), may hold values from -6 to 6
- near_tiles: bfloat16 [32, 7, 512, 512], P(('near', 'row', 'col')), may hold values from -0.09375 to 0.09375
- tile_scales: float32 [32, 7], P(('near', 'row', 'col')), may hold values from 0.3 to 3
- neighbours: int32 [32, 7], P(('near', 'row', 'col')), may hold values from 0 to 31, as said below
- source_cluster_basis: bfloat16 [32, 512, 64], P(('near', 'row', 'col')), may hold values from -0.25 to 0.25
- basis_out: bfloat16 [32, 512, 64], P(('near', 'row', 'col')), may hold values from -0.75 to 0.75
- couplings: bfloat16 [32, 32, 64, 64], P(('near', 'row'), 'col'), may hold values from -0.125 to 0.125
Outputs:
- solution_field: float32 [32, 512, 128], P(('near', 'row', 'col'))
- residual: float32 [32, 512, 128], P(('near', 'row', 'col'))
The draws below stay inside these ranges and needn't reach their ends.
Inputs may be any that keep to these rules, and one draw needn't show every extreme that they name: `neighbours`: row t names 7 different clusters, each within 4 of t in the wrapped cluster order.
All inputs are finite; a program needn't handle non-finite values.
Results may differ from the reference program's by a relative error of at most 0.0051.
Values may be sent and summed in bfloat16 or wider, within the bound.
A program may use at most 64 MiB of HBM per device.

```python
import math
import jax
import jax.numpy as jnp
from jax import lax

LEAF = 512
RANK = 64
RHS = 128
NEIGH = 7
REACH = 4
ITERS = 2
CL_DEV = 1
CLUSTERS = 32
N_COL = 4


def draw_neighbours(key, part):
    spread = 2 * REACH + 1
    scores = jax.random.randint(key, (CLUSTERS, spread), 0, 65536)
    scores = scores * spread + jnp.arange(spread, dtype=jnp.int32)[None, :]
    ignored, picked = lax.top_k(scores, NEIGH)
    anchor_cluster = jnp.arange(CLUSTERS, dtype=jnp.int32)[:, None]
    return jnp.mod(anchor_cluster + picked.astype(jnp.int32) - REACH, CLUSTERS).astype(jnp.int32)


def block_levels(stream_key, dims, shards, least, high):
    factor_of = 1.0
    for position, shards_of in shards:
        steps = jax.random.uniform(jax.random.fold_in(jax.random.fold_in(stream_key, 6), position), (shards_of,), jnp.float32, least / len(shards), high / len(shards))
        factor_of = factor_of * jnp.repeat(jnp.exp(steps), dims[position] // shards_of).reshape((-1,) + (1,) * (len(dims) - 1 - position))
    return factor_of


def centred(key, extent, scale, most, pieces=(), kind=jnp.bfloat16):
    array = scale * jax.random.normal(key, extent, jnp.float32)
    if pieces:
        array = array * block_levels(key, extent, pieces, -0.22, 0.18)
    return jnp.clip(array, -most, most).astype(kind)


def setup_inputs(seed: int = 0) -> dict:
    splits = jax.random.split(jax.random.key(seed), 9)
    return {
        "right_side": centred(splits[0], (CLUSTERS, LEAF, RHS), 1.0, 6.0, ((0, 32),), jnp.float32),
        "start_guess": centred(splits[1], (CLUSTERS, LEAF, RHS), 1.0, 6.0, ((0, 32),), jnp.float32),
        "near_tiles": centred(splits[2], (CLUSTERS, NEIGH, LEAF, LEAF), (NEIGH * LEAF) ** -0.5, 0.09375, ((0, 32),)),
        "tile_scales": jnp.clip(jnp.exp(math.log(3.0) - 2.3025851 * jax.random.uniform(splits[3], (CLUSTERS, NEIGH), jnp.float32) ** block_levels(splits[3], (CLUSTERS, NEIGH), ((0, 32),), -0.2, 0.2)), 0.3, 3.0),
        "neighbours": draw_neighbours(jax.random.fold_in(splits[8], 71), 0),
        "source_cluster_basis": centred(splits[5], (CLUSTERS, LEAF, RANK), LEAF ** -0.5, 0.25, ((0, 32),)),
        "basis_out": centred(splits[6], (CLUSTERS, LEAF, RANK), RANK ** -0.5, 0.75, ((0, 32),)),
        "couplings": centred(splits[7], (CLUSTERS, CLUSTERS, RANK, RANK), (CLUSTERS * RANK) ** -0.5, 0.125, ((0, 8), (1, 4))),
    }


damping = 0.5


def slot_owner(slot_ids):
    per_col = CLUSTERS // N_COL
    within = slot_ids % per_col
    column = slot_ids // per_col
    return (within // CL_DEV * N_COL + column) * CL_DEV + within % CL_DEV


def far_pairs(targets, sources):
    distance = jnp.mod(targets[:, None] - sources[None, :], CLUSTERS)
    return jnp.minimum(distance, CLUSTERS - distance) > REACH


def operate(vector, near_tiles, tile_scales, neighbours, source_cluster_basis, basis_out, couplings):
    coarse_level = vector.astype(jnp.bfloat16)
    expansion_coefficients = jnp.einsum("iao,iau->iou", source_cluster_basis.astype(jnp.float32), coarse_level.astype(jnp.float32),
                       precision=lax.Precision.HIGHEST).astype(jnp.bfloat16)

    def near_one(item):
        tile_set, scale_set, index_set = item
        nearby = jnp.take(coarse_level, index_set, axis=0).astype(jnp.float32)
        basis_products = jnp.einsum("jkl,jlc->jkc", tile_set.astype(jnp.float32), nearby,
                              precision=lax.Precision.HIGHEST)
        return jnp.sum(basis_products * scale_set[:, None, None], axis=0)

    near_term = lax.map(near_one, (near_tiles, tile_scales, neighbours))
    slot_ids = jnp.arange(CLUSTERS, dtype=jnp.int32)
    owners = slot_owner(slot_ids)
    slot_coefs = jnp.take(expansion_coefficients, owners, axis=0).astype(jnp.float32)

    def far_one(item):
        coupling_row, target = item
        admitted = far_pairs(target[None], owners)[0].astype(jnp.float32)
        masked_values = coupling_row.astype(jnp.float32) * admitted[:, None, None]
        return jnp.einsum("mab,mbc->ac", masked_values, slot_coefs, precision=lax.Precision.HIGHEST)

    farfield_coefficients = lax.map(far_one, (couplings, slot_ids))
    far_term = jnp.einsum("cla,cad->cld", basis_out.astype(jnp.float32),
                          farfield_coefficients.astype(jnp.bfloat16).astype(jnp.float32),
                          precision=lax.Precision.HIGHEST)
    return vector + near_term + far_term


def reference(right_side, start_guess, near_tiles, tile_scales, neighbours, source_cluster_basis, basis_out, couplings):
    iterate = start_guess
    residual = right_side
    for sweep in range(ITERS):
        residual = right_side - operate(iterate, near_tiles, tile_scales, neighbours, source_cluster_basis, basis_out, couplings)
        iterate = iterate + damping * residual
    return iterate, residual
```

```python
import functools

import jax
import jax.numpy as jnp
from jax import lax
from jax.experimental import pallas as pl
from jax.experimental.pallas import tpu as pltpu
from jax.sharding import PartitionSpec as P

REACH = 4
ITERS = 2
DAMPING = 0.5
AXES = ("near", "row", "col")
MESH = pl.DeviceIdType.MESH


def kernel(
    sizes,
    neighbours,
    scales,
    right_hbm,
    guess_hbm,
    tiles_hbm,
    source_hbm,
    basis_hbm,
    couplings_hbm,
    x_out,
    residual_out,
    right,
    iterate,
    tiles,
    source,
    basis,
    couplings,
    masked,
    total,
    window,
    coefs,
    parts_out,
    parts_in,
    load_sems,
    halo_send,
    halo_recv,
    coef_send,
    coef_recv,
    part_send,
    part_recv,
):
    n_near, n_row, n_col = sizes
    groups = n_near * n_row
    clusters = groups * n_col
    near, row, col = (lax.axis_index(a) for a in AXES)
    group = near * n_row + row
    me = group * n_col + col
    slots = 2 * REACH + 1
    rank = coefs.shape[2]
    listed = neighbours.shape[1]

    def place(device):
        return (device // (n_row * n_col), device // n_col % n_row, device % n_col)

    def shifted(d):
        return place((me + d + clusters) % clusters)

    def group_peer(i):
        return place((group + i) % groups * n_col + col)

    def col_peer(i):
        return (near, row, (col + i) % n_col)

    loads = [
        pltpu.make_async_copy(src.at[0] if lead else src, dst, load_sems.at[i])
        for i, (src, dst, lead) in enumerate(
            (
                (guess_hbm, iterate, True),
                (source_hbm, source, True),
                (couplings_hbm, couplings, False),
                (tiles_hbm, tiles, True),
                (basis_hbm, basis, True),
                (right_hbm, right, True),
            )
        )
    ]
    for load in loads:
        load.start()

    order = [d for step in range(1, REACH + 1) for d in (step, -step)]
    barrier = pltpu.get_barrier_semaphore()
    for d in order:
        pl.semaphore_signal(barrier, inc=1, device_id=shifted(d), device_id_type=MESH)

    def greet(i, carry):
        pl.semaphore_signal(barrier, inc=1, device_id=group_peer(i), device_id_type=MESH)
        return carry

    lax.fori_loop(1, groups, greet, 0)
    for i in range(1, n_col):
        pl.semaphore_signal(barrier, inc=1, device_id=col_peer(i), device_id_type=MESH)

    choice, weight = [], []
    for j in range(slots):
        pick, scale = jnp.int32(0), jnp.float32(0.0)
        for k in range(listed):
            hit = (neighbours[0, k] - me + REACH + clusters) % clusters == j
            pick = jnp.where(hit, jnp.int32(k), pick)
            scale = jnp.where(hit, scales[0, k], scale)
        choice.append(pick)
        weight.append(scale)

    def coef_copy(sweep, i):
        return pltpu.make_async_remote_copy(
            src_ref=coefs.at[sweep, group],
            dst_ref=coefs.at[sweep, group],
            send_sem=coef_send.at[sweep],
            recv_sem=coef_recv.at[sweep],
            device_id=group_peer(i),
            device_id_type=MESH,
        )

    def halo_copy(sweep, d):
        return pltpu.make_async_remote_copy(
            src_ref=window.at[sweep, REACH],
            dst_ref=window.at[sweep, REACH - d],
            send_sem=halo_send.at[sweep, REACH + d],
            recv_sem=halo_recv.at[sweep, REACH - d],
            device_id=shifted(d),
            device_id_type=MESH,
        )

    def part_copy(sweep, i):
        return pltpu.make_async_remote_copy(
            src_ref=parts_out.at[sweep, i],
            dst_ref=parts_in.at[sweep, i],
            send_sem=part_send.at[sweep, i],
            recv_sem=part_recv.at[sweep, i],
            device_id=col_peer(i),
            device_id_type=MESH,
        )

    def near_product(sweep, j):
        return weight[j] * jnp.dot(
            tiles[choice[j]], window[sweep, j], preferred_element_type=jnp.float32
        )

    loads[0].wait()
    loads[1].wait()
    for sweep in range(ITERS):
        coarse = iterate[...].astype(jnp.bfloat16)
        window[sweep, REACH] = coarse
        coefs[sweep, group] = lax.dot_general(
            source[...], coarse, (((0,), (0,)), ((), ())), preferred_element_type=jnp.float32
        ).astype(jnp.bfloat16)
        if sweep == 0:
            pl.semaphore_wait(barrier, len(order) + groups - 1 + n_col - 1)

        def send(i, carry):
            coef_copy(sweep, i).start()
            return carry

        lax.fori_loop(1, groups, send, 0)
        for d in order:
            halo_copy(sweep, d).start()

        if sweep == 0:
            loads[2].wait()
            for q in range(0, groups, 2):
                sides = []
                for p in (q, q + 1):
                    rows = []
                    for l in range(n_col):
                        distance = (group * n_col + l - (p * n_col + col) + clusters) % clusters
                        far = jnp.minimum(distance, clusters - distance) > REACH
                        rows.append(couplings[l, p].astype(jnp.float32) * far.astype(jnp.float32))
                    sides.append(jnp.concatenate(rows, axis=0).astype(jnp.bfloat16))
                masked[:, q * rank : (q + 2) * rank] = jnp.concatenate(sides, axis=1)
            for load in loads[3:]:
                load.wait()

        total[...] = iterate[...] + near_product(sweep, REACH)

        pltpu.make_async_copy(
            coefs.at[sweep, pl.ds(0, groups - 1)],
            coefs.at[sweep, pl.ds(0, groups - 1)],
            coef_recv.at[sweep],
        ).wait()
        partial = jnp.dot(
            masked[...],
            coefs[sweep].reshape(groups * rank, -1),
            preferred_element_type=jnp.float32,
        ).reshape(n_col, rank, -1)
        for l in range(n_col):
            parts_out[sweep, (l - col + n_col) % n_col] = partial[l].astype(jnp.bfloat16)
        for i in range(1, n_col):
            part_copy(sweep, i).start()

        for d in order[: len(order) // 2]:
            halo_copy(sweep, -d).wait_recv()
            total[...] += near_product(sweep, REACH + d)

        far_coefs = parts_out[sweep, 0].astype(jnp.float32)
        for i in range(1, n_col):
            part_copy(sweep, i).wait_recv()
            far_coefs += parts_in[sweep, i].astype(jnp.float32)
        total[...] += jnp.dot(
            basis[...], far_coefs.astype(jnp.bfloat16), preferred_element_type=jnp.float32
        )

        for d in order[len(order) // 2 :]:
            halo_copy(sweep, -d).wait_recv()
            total[...] += near_product(sweep, REACH + d)

        residual = right[...] - total[...]
        if sweep == ITERS - 1:
            residual_out[0] = residual
            x_out[0] = iterate[...] + DAMPING * residual
        else:
            iterate[...] = iterate[...] + DAMPING * residual

    for sweep in range(ITERS):
        pltpu.make_async_copy(
            coefs.at[sweep, pl.ds(0, groups - 1)],
            coefs.at[sweep, pl.ds(0, groups - 1)],
            coef_send.at[sweep],
        ).wait()
        for d in order:
            halo_copy(sweep, d).wait_send()
        for i in range(1, n_col):
            part_copy(sweep, i).wait_send()


def shards(
    sizes,
    right_side,
    start_guess,
    near_tiles,
    tile_scales,
    neighbours,
    source_cluster_basis,
    basis_out,
    couplings,
):
    local_count, leaf, rhs = right_side.shape
    targets, groups, rank, _ = couplings.shape
    assert local_count == 1 and targets == sizes[2]
    listed = near_tiles.shape[1]
    any_spec = pl.BlockSpec(memory_space=pl.ANY)
    small = pl.BlockSpec(memory_space=pltpu.SMEM)
    vmem = pl.BlockSpec(memory_space=pltpu.VMEM)
    slots = 2 * REACH + 1
    bf16, f32 = jnp.bfloat16, jnp.float32
    dma = pltpu.SemaphoreType.DMA
    return pl.pallas_call(
        functools.partial(kernel, sizes),
        out_shape=[jax.ShapeDtypeStruct(right_side.shape, f32)] * 2,
        in_specs=[small] * 2 + [any_spec] * 6,
        out_specs=[vmem] * 2,
        scratch_shapes=[
            pltpu.VMEM((leaf, rhs), f32),
            pltpu.VMEM((leaf, rhs), f32),
            pltpu.VMEM((listed, leaf, leaf), bf16),
            pltpu.VMEM((leaf, rank), bf16),
            pltpu.VMEM((leaf, rank), bf16),
            pltpu.VMEM(couplings.shape, bf16),
            pltpu.VMEM((targets * rank, groups * rank), bf16),
            pltpu.VMEM((leaf, rhs), f32),
            pltpu.VMEM((ITERS, slots, leaf, rhs), bf16),
            pltpu.VMEM((ITERS, groups, rank, rhs), bf16),
            pltpu.VMEM((ITERS, targets, rank, rhs), bf16),
            pltpu.VMEM((ITERS, targets, rank, rhs), bf16),
            dma((6,)),
            dma((ITERS, slots)),
            dma((ITERS, slots)),
            dma((ITERS,)),
            dma((ITERS,)),
            dma((ITERS, targets)),
            dma((ITERS, targets)),
        ],
        compiler_params=pltpu.CompilerParams(collective_id=0, has_side_effects=True),
    )(
        neighbours,
        tile_scales,
        right_side,
        start_guess,
        near_tiles,
        source_cluster_basis,
        basis_out,
        couplings,
    )


def solution(mesh):
    sizes = tuple(mesh.shape[a] for a in AXES)
    lead = P(AXES, None, None)
    in_specs = (
        lead,
        lead,
        P(AXES, None, None, None),
        P(AXES, None),
        P(AXES, None),
        lead,
        lead,
        P(("near", "row"), "col", None, None),
    )
    body = functools.partial(shards, sizes)
    return jax.shard_map(
        body, mesh=mesh, in_specs=in_specs, out_specs=(lead, lead), check_vma=False
    )
```

```python
import functools

import jax
import jax.numpy as jnp
from jax import lax
from jax.experimental import pallas as pl
from jax.experimental.pallas import tpu as pltpu
from jax.sharding import PartitionSpec as P

REACH = 4
ITERS = 2
DAMPING = 0.5
AXES = ("near", "row", "col")
MESH = pl.DeviceIdType.MESH


def kernel(
    sizes,
    neighbours,
    scales,
    right_hbm,
    guess_hbm,
    tiles_hbm,
    source_hbm,
    basis_hbm,
    couplings_hbm,
    last,
    applied,
    right,
    iterate,
    tiles,
    source,
    basis,
    couplings,
    masked,
    total,
    window,
    coefs,
    parts_out,
    parts_in,
    load_sems,
    halo_send,
    halo_recv,
    coef_send,
    coef_recv,
    part_send,
    part_recv,
):
    n_near, n_row, n_col = sizes
    groups = n_near * n_row
    clusters = groups * n_col
    near, row, col = (lax.axis_index(a) for a in AXES)
    group = near * n_row + row
    me = group * n_col + col
    slots = 2 * REACH + 1
    rank = coefs.shape[2]
    listed = neighbours.shape[1]

    def place(device):
        return (device // (n_row * n_col), device // n_col % n_row, device % n_col)

    def group_peer(i):
        return place((group + i) % groups * n_col + col)

    def col_peer(i):
        return (near, row, (col + i) % n_col)

    loads = [
        pltpu.make_async_copy(src.at[0] if lead else src, dst, load_sems.at[i])
        for i, (src, dst, lead) in enumerate(
            (
                (guess_hbm, iterate, True),
                (source_hbm, source, True),
                (couplings_hbm, couplings, False),
                (tiles_hbm, tiles, True),
                (basis_hbm, basis, True),
                (right_hbm, right, True),
            )
        )
    ]
    for load in loads:
        load.start()

    barrier = pltpu.get_barrier_semaphore()
    def greet(i, carry):
        pl.semaphore_signal(barrier, inc=1, device_id=group_peer(i), device_id_type=MESH)
        return carry

    lax.fori_loop(1, groups, greet, 0)
    for i in range(1, n_col):
        pl.semaphore_signal(barrier, inc=1, device_id=col_peer(i), device_id_type=MESH)

    offsets = [
        (neighbours[0, k] - me + REACH + clusters) % clusters - REACH for k in range(listed)
    ]
    side = 1 - col // (n_col // 2) * 2
    parity = col % 2 * 2 - 1
    ahead = place((me + n_col) % clusters)
    behind = place((me + clusters - n_col) % clusters)
    across = place(me + 2 * side)
    partner = place(me - parity)

    def coef_copy(sweep, i):
        return pltpu.make_async_remote_copy(
            src_ref=coefs.at[sweep, group],
            dst_ref=coefs.at[sweep, group],
            send_sem=coef_send.at[sweep],
            recv_sem=coef_recv.at[sweep],
            device_id=group_peer(i),
            device_id_type=MESH,
        )

    def halo_copy(sweep, number, block, target, lands):
        return pltpu.make_async_remote_copy(
            src_ref=window.at[sweep, REACH + block],
            dst_ref=window.at[sweep, REACH + lands],
            send_sem=halo_send.at[sweep, number],
            recv_sem=halo_recv.at[sweep, REACH + lands],
            device_id=target,
            device_id_type=MESH,
        )

    def halo_wait(sweep, d):
        pltpu.make_async_copy(
            window.at[sweep, REACH + d], window.at[sweep, REACH + d], halo_recv.at[sweep, REACH + d]
        ).wait()

    def part_copy(sweep, i):
        return pltpu.make_async_remote_copy(
            src_ref=parts_out.at[sweep, i],
            dst_ref=parts_in.at[sweep, i],
            send_sem=part_send.at[sweep, i],
            recv_sem=part_recv.at[sweep, i],
            device_id=col_peer(i),
            device_id_type=MESH,
        )

    def near_product(sweep, d):
        pick, scale = jnp.int32(0), jnp.float32(0.0)
        for k in range(listed):
            hit = offsets[k] == d
            pick = jnp.where(hit, jnp.int32(k), pick)
            scale = jnp.where(hit, scales[0, k], scale)
        return scale * jnp.dot(
            tiles[pick], window[sweep, REACH + d], preferred_element_type=jnp.float32
        )

    def add_near(sweep, d):
        total[...] += near_product(sweep, d)

    def copies(sweep):
        return [
            halo_copy(sweep, 0, 0, ahead, -n_col),
            halo_copy(sweep, 1, 0, behind, n_col),
            halo_copy(sweep, 2, 0, across, -2 * side),
            halo_copy(sweep, 3, 0, partner, parity),
            halo_copy(sweep, 4, n_col * side, across, 2 * side),
            halo_copy(sweep, 5, 2 * side, partner, 2 * side + parity),
            halo_copy(sweep, 6, -n_col * parity, partner, -3 * parity),
            halo_copy(sweep, 7, -2 * side, partner, -2 * side + parity),
        ]

    loads[0].wait()
    loads[1].wait()
    for sweep in range(ITERS):
        coarse = iterate[...].astype(jnp.bfloat16)
        window[sweep, REACH] = coarse
        coefs[sweep, group] = lax.dot_general(
            source[...], coarse, (((1,), (0,)), ((), ())), preferred_element_type=jnp.float32
        ).astype(jnp.bfloat16)
        if sweep == 0:
            pl.semaphore_wait(barrier, groups - 1 + n_col - 1)

        def send(i, carry):
            coef_copy(sweep, i).start()
            return carry

        lax.fori_loop(1, groups, send, 0)
        halo = copies(sweep)
        for copy in halo[:4]:
            copy.start()

        if sweep == 0:
            loads[2].wait()
            for q in range(0, groups, 2):
                sides = []
                for p in (q, q + 1):
                    rows = []
                    for l in range(n_col):
                        distance = (group * n_col + l - (p * n_col + col) + clusters) % clusters
                        far = jnp.minimum(distance, clusters - distance) > REACH
                        rows.append(couplings[l, p].astype(jnp.float32) * far.astype(jnp.float32))
                    sides.append(jnp.concatenate(rows, axis=0).astype(jnp.bfloat16))
                masked[:, q * rank : (q + 2) * rank] = jnp.concatenate(sides, axis=1)
            for load in loads[3:]:
                load.wait()

        total[...] = iterate[...] + near_product(sweep, 0)
        halo_wait(sweep, 2 * side)
        halo[5].start()
        add_near(sweep, 2 * side)
        halo_wait(sweep, -parity)
        add_near(sweep, -parity)

        pltpu.make_async_copy(
            coefs.at[sweep, pl.ds(0, groups - 1)],
            coefs.at[sweep, pl.ds(0, groups - 1)],
            coef_recv.at[sweep],
        ).wait()
        partial = jnp.dot(
            masked[...],
            coefs[sweep].reshape(groups * rank, -1),
            preferred_element_type=jnp.float32,
        ).reshape(n_col, rank, -1)
        for l in range(n_col):
            parts_out[sweep, (l - col + n_col) % n_col] = partial[l].astype(jnp.bfloat16)
        for i in range(1, n_col):
            part_copy(sweep, i).start()

        halo_wait(sweep, n_col * side)
        halo[4].start()

        @pl.when(parity == -side)
        def _():
            halo[6].start()

        add_near(sweep, n_col * side)
        halo_wait(sweep, -n_col * side)

        @pl.when(parity == side)
        def _():
            halo[6].start()

        add_near(sweep, -n_col * side)
        halo_wait(sweep, 2 * side - parity)
        add_near(sweep, 2 * side - parity)

        far_coefs = parts_out[sweep, 0].astype(jnp.float32)
        for i in range(1, n_col):
            part_copy(sweep, i).wait_recv()
            far_coefs += parts_in[sweep, i].astype(jnp.float32)
        total[...] += lax.dot_general(
            basis[...],
            far_coefs.astype(jnp.bfloat16),
            (((0,), (0,)), ((), ())),
            preferred_element_type=jnp.float32,
        )

        halo_wait(sweep, -2 * side)
        halo[7].start()
        add_near(sweep, -2 * side)
        for d in (3 * parity, -2 * side - parity):
            halo_wait(sweep, d)
            add_near(sweep, d)

        if sweep == ITERS - 1:
            applied[0] = total[...]
            last[0] = iterate[...]
        else:
            iterate[...] = iterate[...] + DAMPING * (right[...] - total[...])

    for sweep in range(ITERS):
        pltpu.make_async_copy(
            coefs.at[sweep, pl.ds(0, groups - 1)],
            coefs.at[sweep, pl.ds(0, groups - 1)],
            coef_send.at[sweep],
        ).wait()
        for copy in copies(sweep):
            copy.wait_send()
        for i in range(1, n_col):
            part_copy(sweep, i).wait_send()


def shards(
    sizes,
    right_side,
    start_guess,
    near_tiles,
    tile_scales,
    neighbours,
    source_cluster_basis,
    basis_out,
    couplings,
):
    local_count, leaf, rhs = right_side.shape
    targets, groups, rank, _ = couplings.shape
    assert local_count == 1 and targets == sizes[2] == REACH
    listed = near_tiles.shape[1]
    any_spec = pl.BlockSpec(memory_space=pl.ANY)
    small = pl.BlockSpec(memory_space=pltpu.SMEM)
    vmem = pl.BlockSpec(memory_space=pltpu.VMEM)
    slots = 2 * REACH + 1
    bf16, f32 = jnp.bfloat16, jnp.float32
    dma = pltpu.SemaphoreType.DMA
    last, applied = pl.pallas_call(
        functools.partial(kernel, sizes),
        out_shape=[jax.ShapeDtypeStruct(right_side.shape, f32)] * 2,
        in_specs=[small] * 2 + [any_spec] * 6,
        out_specs=[vmem] * 2,
        scratch_shapes=[
            pltpu.VMEM((leaf, rhs), f32),
            pltpu.VMEM((leaf, rhs), f32),
            pltpu.VMEM((listed, leaf, leaf), bf16),
            pltpu.VMEM((rank, leaf), bf16),
            pltpu.VMEM((rank, leaf), bf16),
            pltpu.VMEM(couplings.shape, bf16),
            pltpu.VMEM((targets * rank, groups * rank), bf16),
            pltpu.VMEM((leaf, rhs), f32),
            pltpu.VMEM((ITERS, slots, leaf, rhs), bf16),
            pltpu.VMEM((ITERS, groups, rank, rhs), bf16),
            pltpu.VMEM((ITERS, targets, rank, rhs), bf16),
            pltpu.VMEM((ITERS, targets, rank, rhs), bf16),
            dma((6,)),
            dma((ITERS, 8)),
            dma((ITERS, slots)),
            dma((ITERS,)),
            dma((ITERS,)),
            dma((ITERS, targets)),
            dma((ITERS, targets)),
        ],
        compiler_params=pltpu.CompilerParams(collective_id=0, has_side_effects=True),
    )(
        neighbours,
        tile_scales,
        right_side,
        start_guess,
        near_tiles,
        jnp.swapaxes(source_cluster_basis, 1, 2),
        jnp.swapaxes(basis_out, 1, 2),
        couplings,
    )
    residual = right_side - applied
    return last + DAMPING * residual, residual


def solution(mesh):
    sizes = tuple(mesh.shape[a] for a in AXES)
    lead = P(AXES, None, None)
    in_specs = (
        lead,
        lead,
        P(AXES, None, None, None),
        P(AXES, None),
        P(AXES, None),
        lead,
        lead,
        P(("near", "row"), "col", None, None),
    )
    body = functools.partial(shards, sizes)
    return jax.shard_map(
        body, mesh=mesh, in_specs=in_specs, out_specs=(lead, lead), check_vma=False
    )
```

```python
import functools

import jax
import jax.numpy as jnp
from jax import lax
from jax.experimental import pallas as pl
from jax.experimental.pallas import tpu as pltpu
from jax.sharding import PartitionSpec as P

REACH = 4
ITERS = 2
CHUNKS = 4
DAMPING = 0.5
AXES = ("near", "row", "col")
MESH = pl.DeviceIdType.MESH


def kernel(
    sizes,
    neighbours,
    scales,
    right_hbm,
    guess_hbm,
    tiles_hbm,
    source_hbm,
    basis_hbm,
    couplings_hbm,
    last,
    applied,
    right,
    iterate,
    tiles,
    source,
    basis,
    couplings,
    masked,
    total,
    window,
    coefs,
    parts_out,
    parts_in,
    load_sems,
    halo_send,
    halo_recv,
    coef_send,
    coef_recv,
    part_send,
    part_recv,
):
    n_near, n_row, n_col = sizes
    groups = n_near * n_row
    clusters = groups * n_col
    near, row, col = (lax.axis_index(a) for a in AXES)
    group = near * n_row + row
    me = group * n_col + col
    slots = 2 * REACH + 1
    rank = coefs.shape[2]
    listed = neighbours.shape[1]

    def place(device):
        return (device // (n_row * n_col), device // n_col % n_row, device % n_col)

    def group_peer(i):
        return place((group + i) % groups * n_col + col)

    def col_peer(i):
        return (near, row, (col + i) % n_col)

    loads = [
        pltpu.make_async_copy(src.at[0] if lead else src, dst, load_sems.at[i])
        for i, (src, dst, lead) in enumerate(
            (
                (guess_hbm, iterate, True),
                (source_hbm, source, True),
                (couplings_hbm, couplings, False),
                (tiles_hbm, tiles, True),
                (basis_hbm, basis, True),
                (right_hbm, right, True),
            )
        )
    ]
    for load in loads:
        load.start()

    barrier = pltpu.get_barrier_semaphore()
    def greet(i, carry):
        pl.semaphore_signal(barrier, inc=1, device_id=group_peer(i), device_id_type=MESH)
        return carry

    lax.fori_loop(1, groups, greet, 0)
    for i in range(1, n_col):
        pl.semaphore_signal(barrier, inc=1, device_id=col_peer(i), device_id_type=MESH)

    offsets = [
        (neighbours[0, k] - me + REACH + clusters) % clusters - REACH for k in range(listed)
    ]
    side = 1 - col // (n_col // 2) * 2
    parity = col % 2 * 2 - 1
    ahead = place((me + n_col) % clusters)
    behind = place((me + clusters - n_col) % clusters)
    across = place(me + 2 * side)
    partner = place(me - parity)

    def row_copy(sweep, i):
        return pltpu.make_async_remote_copy(
            src_ref=coefs.at[sweep, group],
            dst_ref=coefs.at[sweep, group],
            send_sem=coef_send.at[sweep, 0],
            recv_sem=coef_recv.at[sweep, 0],
            device_id=(near, (row + i) % n_row, col),
            device_id_type=MESH,
        )

    def near_copy(sweep, i):
        mine = pl.ds(near * n_row, n_row)
        return pltpu.make_async_remote_copy(
            src_ref=coefs.at[sweep, mine],
            dst_ref=coefs.at[sweep, mine],
            send_sem=coef_send.at[sweep, 1],
            recv_sem=coef_recv.at[sweep, 1],
            device_id=((near + i) % n_near, row, col),
            device_id_type=MESH,
        )

    def coef_wait(sems, sweep, stage):
        count = groups - n_row if stage else n_row - 1
        part = coefs.at[sweep, pl.ds(0, count)]
        pltpu.make_async_copy(part, part, sems.at[sweep, stage]).wait()

    rows = window.shape[2] // CHUNKS

    def halo_copy(sweep, number, block, target, lands, c):
        span = pl.ds(c * rows, rows)
        return pltpu.make_async_remote_copy(
            src_ref=window.at[sweep, REACH + block, span],
            dst_ref=window.at[sweep, REACH + lands, span],
            send_sem=halo_send.at[sweep, number, c],
            recv_sem=halo_recv.at[sweep, REACH + lands, c],
            device_id=target,
            device_id_type=MESH,
        )

    def halo_wait(sweep, d, chunks=range(CHUNKS)):
        for c in chunks:
            piece = window.at[sweep, REACH + d, pl.ds(c * rows, rows)]
            pltpu.make_async_copy(piece, piece, halo_recv.at[sweep, REACH + d, c]).wait()

    def part_copy(sweep, i):
        return pltpu.make_async_remote_copy(
            src_ref=parts_out.at[sweep, i],
            dst_ref=parts_in.at[sweep, i],
            send_sem=part_send.at[sweep, i],
            recv_sem=part_recv.at[sweep, i],
            device_id=col_peer(i),
            device_id_type=MESH,
        )

    def near_product(sweep, d):
        pick, scale = jnp.int32(0), jnp.float32(0.0)
        for k in range(listed):
            hit = offsets[k] == d
            pick = jnp.where(hit, jnp.int32(k), pick)
            scale = jnp.where(hit, scales[0, k], scale)
        return scale * jnp.dot(
            tiles[pick], window[sweep, REACH + d], preferred_element_type=jnp.float32
        )

    def add_near(sweep, d):
        total[...] += near_product(sweep, d)

    routes = [
        (0, 0, ahead, -n_col),
        (1, 0, behind, n_col),
        (2, 0, across, -2 * side),
        (3, 0, partner, parity),
        (4, n_col * side, across, 2 * side),
        (5, 2 * side, partner, 2 * side + parity),
        (6, -n_col * parity, partner, -3 * parity),
        (7, -2 * side, partner, -2 * side + parity),
    ]

    loads[0].wait()
    loads[1].wait()
    for sweep in range(ITERS):
        coarse = iterate[...].astype(jnp.bfloat16)
        window[sweep, REACH] = coarse
        coefs[sweep, group] = lax.dot_general(
            source[...], coarse, (((1,), (0,)), ((), ())), preferred_element_type=jnp.float32
        ).astype(jnp.bfloat16)
        if sweep == 0:
            pl.semaphore_wait(barrier, groups - 1 + n_col - 1)

        for i in range(1, n_row):
            row_copy(sweep, i).start()
        for c in range(CHUNKS):
            for route in routes[:4]:
                halo_copy(sweep, *route, c).start()

        if sweep == 0:
            loads[2].wait()
            for q in range(0, groups, 2):
                sides = []
                for p in (q, q + 1):
                    stack = []
                    for l in range(n_col):
                        distance = (group * n_col + l - (p * n_col + col) + clusters) % clusters
                        far = jnp.minimum(distance, clusters - distance) > REACH
                        stack.append(couplings[l, p].astype(jnp.float32) * far.astype(jnp.float32))
                    sides.append(jnp.concatenate(stack, axis=0).astype(jnp.bfloat16))
                masked[:, q * rank : (q + 2) * rank] = jnp.concatenate(sides, axis=1)
            for load in loads[3:]:
                load.wait()

        total[...] = iterate[...] + near_product(sweep, 0)
        halo_wait(sweep, -parity)
        add_near(sweep, -parity)

        coef_wait(coef_recv, sweep, 0)

        def pass_on(i, carry):
            near_copy(sweep, i).start()
            return carry

        lax.fori_loop(1, n_near, pass_on, 0)
        for c in range(CHUNKS):
            halo_wait(sweep, 2 * side, (c,))
            halo_copy(sweep, *routes[5], c).start()
        add_near(sweep, 2 * side)
        coef_wait(coef_recv, sweep, 1)
        partial = jnp.dot(
            masked[...],
            coefs[sweep].reshape(groups * rank, -1),
            preferred_element_type=jnp.float32,
        ).reshape(n_col, rank, -1)
        for l in range(n_col):
            parts_out[sweep, (l - col + n_col) % n_col] = partial[l].astype(jnp.bfloat16)
        for i in range(1, n_col):
            part_copy(sweep, i).start()

        for c in range(CHUNKS):
            halo_wait(sweep, n_col * side, (c,))
            halo_copy(sweep, *routes[4], c).start()

            @pl.when(parity == -side)
            def _():
                halo_copy(sweep, *routes[6], c).start()

        add_near(sweep, n_col * side)
        for c in range(CHUNKS):
            halo_wait(sweep, -n_col * side, (c,))

            @pl.when(parity == side)
            def _():
                halo_copy(sweep, *routes[6], c).start()

        add_near(sweep, -n_col * side)
        halo_wait(sweep, 2 * side - parity)
        add_near(sweep, 2 * side - parity)

        far_coefs = parts_out[sweep, 0].astype(jnp.float32)
        for i in range(1, n_col):
            part_copy(sweep, i).wait_recv()
            far_coefs += parts_in[sweep, i].astype(jnp.float32)
        total[...] += lax.dot_general(
            basis[...],
            far_coefs.astype(jnp.bfloat16),
            (((0,), (0,)), ((), ())),
            preferred_element_type=jnp.float32,
        )

        for c in range(CHUNKS):
            halo_wait(sweep, -2 * side, (c,))
            halo_copy(sweep, *routes[7], c).start()
        add_near(sweep, -2 * side)
        for d in (3 * parity, -2 * side - parity):
            halo_wait(sweep, d)
            add_near(sweep, d)

        if sweep == ITERS - 1:
            applied[0] = total[...]
            last[0] = iterate[...]
        else:
            iterate[...] = iterate[...] + DAMPING * (right[...] - total[...])

    for sweep in range(ITERS):
        coef_wait(coef_send, sweep, 0)
        coef_wait(coef_send, sweep, 1)
        for route in routes:
            for c in range(CHUNKS):
                halo_copy(sweep, *route, c).wait_send()
        for i in range(1, n_col):
            part_copy(sweep, i).wait_send()


def shards(
    sizes,
    right_side,
    start_guess,
    near_tiles,
    tile_scales,
    neighbours,
    source_cluster_basis,
    basis_out,
    couplings,
):
    local_count, leaf, rhs = right_side.shape
    targets, groups, rank, _ = couplings.shape
    assert local_count == 1 and targets == sizes[2] == REACH
    listed = near_tiles.shape[1]
    any_spec = pl.BlockSpec(memory_space=pl.ANY)
    small = pl.BlockSpec(memory_space=pltpu.SMEM)
    vmem = pl.BlockSpec(memory_space=pltpu.VMEM)
    slots = 2 * REACH + 1
    bf16, f32 = jnp.bfloat16, jnp.float32
    dma = pltpu.SemaphoreType.DMA
    last, applied = pl.pallas_call(
        functools.partial(kernel, sizes),
        out_shape=[jax.ShapeDtypeStruct(right_side.shape, f32)] * 2,
        in_specs=[small] * 2 + [any_spec] * 6,
        out_specs=[vmem] * 2,
        scratch_shapes=[
            pltpu.VMEM((leaf, rhs), f32),
            pltpu.VMEM((leaf, rhs), f32),
            pltpu.VMEM((listed, leaf, leaf), bf16),
            pltpu.VMEM((rank, leaf), bf16),
            pltpu.VMEM((rank, leaf), bf16),
            pltpu.VMEM(couplings.shape, bf16),
            pltpu.VMEM((targets * rank, groups * rank), bf16),
            pltpu.VMEM((leaf, rhs), f32),
            pltpu.VMEM((ITERS, slots, leaf, rhs), bf16),
            pltpu.VMEM((ITERS, groups, rank, rhs), bf16),
            pltpu.VMEM((ITERS, targets, rank, rhs), bf16),
            pltpu.VMEM((ITERS, targets, rank, rhs), bf16),
            dma((6,)),
            dma((ITERS, 8, CHUNKS)),
            dma((ITERS, slots, CHUNKS)),
            dma((ITERS, 2)),
            dma((ITERS, 2)),
            dma((ITERS, targets)),
            dma((ITERS, targets)),
        ],
        compiler_params=pltpu.CompilerParams(collective_id=0, has_side_effects=True),
    )(
        neighbours,
        tile_scales,
        right_side,
        start_guess,
        near_tiles,
        jnp.swapaxes(source_cluster_basis, 1, 2),
        jnp.swapaxes(basis_out, 1, 2),
        couplings,
    )
    residual = right_side - applied
    return last + DAMPING * residual, residual


def solution(mesh):
    sizes = tuple(mesh.shape[a] for a in AXES)
    lead = P(AXES, None, None)
    in_specs = (
        lead,
        lead,
        P(AXES, None, None, None),
        P(AXES, None),
        P(AXES, None),
        lead,
        lead,
        P(("near", "row"), "col", None, None),
    )
    body = functools.partial(shards, sizes)
    return jax.shard_map(
        body, mesh=mesh, in_specs=in_specs, out_specs=(lead, lead), check_vma=False
    )
```
